32 devices in a mesh: blk: 8 (over z, x), sub: 4 (over y, core).
Axes of the slice: x: 2, y: 2, z: 4, core: 2. Of those that a mesh axis runs over, the one named last changes fastest.
Arguments:
- features: float32 [16384, 128], P(('blk', 'sub')), may hold values from -6 to 6
- weight: float32 [128, 128], replicated, may hold values from -0.5 to 0.5
- bias: float32 [128], replicated, may hold values from -3 to 3
- adj_tiles: float32 [512, 128, 128], P(('blk', 'sub')), may hold values from 0 to 0.046875
- tile_rows: int32 [512], P(('blk', 'sub')), may hold values from 0 to 127, as said below
- tile_cols: int32 [512], P(('blk', 'sub')), may hold values from 0 to 127, as said below
- tile_counts: int32 [256], P(('blk', 'sub')), may hold values from 0 to 2, as said below
- cotangent: float32 [16384, 128], P(('blk', 'sub')), may hold values from -6 to 6
Outputs:
- activation: float32 [16384, 128], P(('blk', 'sub'))
- grad_features: float32 [16384, 128], P(('blk', 'sub'))
- grad_weight: float32 [128, 128], replicated
- grad_bias: float32 [128], replicated
The draws below stay inside these ranges and needn't reach their ends.
Inputs may be any that keep to these rules, and one draw needn't show every extreme that they name: `tile_rows`: a slot's row block is one of the 16 blocks of the 4 devices that share the holding device's blk index. `tile_cols`: slot k of a device has its column block in group k // 2, the 16 blocks of the devices with blk index k // 2. `tile_counts`: the live slots of a group are its first ones; some device has all slots live in every draw.
All inputs are finite; a program needn't handle non-finite values.
Results may differ from the reference program's by a relative error of at most 0.00023.
Values sent between devices are 32-bit elements; how exact they have to be, the bound alone decides.
No kernel may reach another device: no remote copies, remote signals or barrier semaphores. Data moves between devices by JAX's collectives and lax.ppermute only.
A program may use at most 128 MiB of HBM per device.

```python
import math
import jax
import jax.numpy as jnp
from jax import lax

FEAT = 128
BS = 128
CAP = 2
GROUP_BLOCKS = 16
SLOTS = 16
NODES = 16384
TILES = 512
N_BLK = 8
N_SUB = 4
DEVICES = 32


def draw_tile_rows(key, part):
    index = jnp.arange(TILES, dtype=jnp.int32)
    group = index // SLOTS // N_SUB
    offset = jax.random.randint(jax.random.fold_in(key, 11), (TILES,), 0, GROUP_BLOCKS)
    return (group * GROUP_BLOCKS + offset).astype(jnp.int32)


def draw_tile_cols(key, part):
    index = jnp.arange(TILES, dtype=jnp.int32)
    group = index % SLOTS // CAP
    offset = jax.random.randint(jax.random.fold_in(key, 23), (TILES,), 0, GROUP_BLOCKS)
    return (group * GROUP_BLOCKS + offset).astype(jnp.int32)


def draw_tile_counts(key, part):
    index = jnp.arange(DEVICES * N_BLK, dtype=jnp.int32)
    device = index // N_BLK
    levels = jax.random.randint(jax.random.fold_in(key, 37), (DEVICES,), 0, 4)
    busy = (levels == 0) | (jnp.arange(DEVICES, dtype=jnp.int32) == 0)
    spread = jax.random.randint(jax.random.fold_in(key, 41), (DEVICES * N_BLK,), 0, CAP + 1)
    return jnp.where(busy[device], CAP, spread).astype(jnp.int32)


def block_scale(key, extent, split, least, high):
    def one(axis_at, shards_of):
        heights = jax.random.uniform(jax.random.fold_in(jax.random.fold_in(key, 6), axis_at), (shards_of,), jnp.float32, least / len(split), high / len(split))
        return jnp.repeat(jnp.exp(heights), extent[axis_at] // shards_of).reshape((-1,) + (1,) * (len(extent) - axis_at - 1))

    loudness = one(*split[0])
    for cut in split[1:]:
        loudness = loudness * one(*cut)
    return loudness


def noise(stream_key, shape, scale, reach, split=(), kind=jnp.bfloat16):
    values = scale * jax.random.normal(stream_key, shape, jnp.float32)
    if split:
        values = values * block_scale(stream_key, shape, split, -0.22, 0.18)
    return jnp.clip(values, -reach, reach).astype(kind)


def setup_inputs(seed: int = 0) -> dict:
    seeds = jax.random.split(jax.random.key(seed), 9)
    features = noise(seeds[0], (NODES, FEAT), 1.0, 6.0, ((0, 32),), jnp.float32)
    weight = noise(seeds[1], (FEAT, FEAT), FEAT ** -0.5, 0.5, (), jnp.float32)
    bias = noise(seeds[2], (FEAT,), 0.5, 3.0, (), jnp.float32)
    adj_tiles = jnp.clip(0.046875 * jax.random.uniform(seeds[3], (TILES, BS, BS), jnp.float32) ** block_scale(seeds[3], (TILES, BS, BS), ((0, 32),), -0.2, 0.2), 0.0, 0.046875)
    tile_rows = draw_tile_rows(jax.random.fold_in(seeds[8], 71), 0)
    tile_cols = draw_tile_cols(jax.random.fold_in(seeds[8], 71), 0)
    tile_counts = draw_tile_counts(jax.random.fold_in(seeds[8], 71), 0)
    cotangent = noise(seeds[7], (NODES, FEAT), 1.0, 6.0, ((0, 32),), jnp.float32)
    return dict(features=features, weight=weight, bias=bias, adj_tiles=adj_tiles, tile_rows=tile_rows, tile_cols=tile_cols, tile_counts=tile_counts, cotangent=cotangent)


def aggregate(values, adj_tiles, tile_rows, tile_cols, tile_counts):
    width = values.shape[1]
    blocked = values.reshape(-1, BS, width)
    slot_ids = jnp.arange(SLOTS, dtype=jnp.int32)
    counts_view = tile_counts.reshape(DEVICES, N_BLK)
    alive = ((slot_ids % CAP)[None, :] < counts_view[:, slot_ids // CAP]).astype(values.dtype)
    tiles_view = adj_tiles.reshape(DEVICES, SLOTS, BS, BS)
    rows_view = tile_rows.reshape(DEVICES, SLOTS)
    cols_view = tile_cols.reshape(DEVICES, SLOTS)

    def one_device(summed, pieces):
        tiles_here, rows_here, cols_here, alive_here = pieces
        masked = tiles_here * alive_here[:, None, None]
        pulled = jnp.einsum('kij,kjf->kif', masked, blocked[cols_here], precision=lax.Precision.HIGHEST)
        pushed = jnp.einsum('kji,kjf->kif', masked, blocked[rows_here], precision=lax.Precision.HIGHEST)
        summed = summed.at[rows_here].add(pulled)
        summed = summed.at[cols_here].add(pushed)
        return (summed, None)
    start = jnp.zeros(blocked.shape, values.dtype)
    summed, _ = lax.scan(one_device, start, (tiles_view, rows_view, cols_view, alive))
    return summed.reshape(values.shape)

def reference(features, weight, bias, adj_tiles, tile_rows, tile_cols, tile_counts, cotangent):
    scale = 1.0 / math.sqrt(NODES)
    mixed = jnp.dot(features, weight, precision=lax.Precision.HIGHEST)
    pre = aggregate(mixed, adj_tiles, tile_rows, tile_cols, tile_counts) + bias
    sigma = jax.nn.sigmoid(pre)
    activation = pre * sigma
    grad_pre = cotangent * sigma * (1.0 + pre * (1.0 - sigma))
    grad_mixed = aggregate(grad_pre, adj_tiles, tile_rows, tile_cols, tile_counts)
    grad_features = jnp.dot(grad_mixed, weight.T, precision=lax.Precision.HIGHEST)
    grad_weight = jnp.dot(features.T, grad_mixed, precision=lax.Precision.HIGHEST) * scale
    grad_bias = lax.optimization_barrier(jnp.sum(grad_pre, axis=0)) * scale
    return (activation, grad_features, grad_weight, grad_bias)
```

```python
import functools
import math

import jax
import jax.numpy as jnp
from jax import lax
from jax.experimental import pallas as pl
from jax.experimental.pallas import tpu as pltpu
from jax.sharding import PartitionSpec as P

BS = 128
CAP = 2
PAD = 8
HIGHEST = lax.Precision.HIGHEST
VMEM = pl.BlockSpec(memory_space=pltpu.VMEM)
SMEM = pl.BlockSpec(memory_space=pltpu.SMEM)
F32 = jnp.float32


def dot(a, b, dims):
    return lax.dot_general(a, b, (dims, ((), ())), precision=HIGHEST, preferred_element_type=F32)


def swap(value, axis, flip):
    n = lax.axis_size(axis)
    return lax.ppermute(value, axis, [(i, i ^ flip) for i in range(n)])


def rows_of(index, size=BS):
    return pl.ds(pl.multiple_of(index * size, size), size)


def send_kernel(n_blk, n_sub, extra, here, rows, counts, wanted, tiles, *refs):
    blocks = refs[:n_sub]
    parts = refs[n_sub : 2 * n_sub] if extra else ()
    outs = refs[-n_blk - 2 : -2] if extra else refs[-n_blk - 1 : -1]
    scratch = refs[-2] if extra else refs[-1]
    blk, sub = here[0], here[1]
    own = blocks[0].shape[0]
    group = own // BS * n_sub
    for j in range(n_sub):
        scratch[rows_of(j ^ sub, own)] = blocks[j][...]
    if extra:
        summed = refs[-1]
        for j in range(n_sub):
            summed[j ^ sub] = parts[j][...]
        total = summed[0]
        for j in range(1, n_sub):
            total = total + summed[j]
    for d in range(n_blk):
        peer = blk ^ d
        for c in range(CAP):
            ask = wanted[peer * CAP + c] - blk * group
            outs[d][c * BS : (c + 1) * BS] = scratch[rows_of(ask)]
            slot = peer * CAP + c
            alive = jnp.where(c < counts[peer], 1.0, 0.0).astype(F32)
            row = rows[slot] - blk * group
            product = dot(tiles[slot] * alive, scratch[rows_of(row)], ((0,), (0,)))
            outs[d][(CAP + c) * BS : (CAP + c + 1) * BS] = product
        if extra:
            outs[d][2 * CAP * BS :] = total


def sum_kernel(n_blk, n_sub, extra, here, rows, counts, wanted, tiles, *refs):
    arrived = refs[:n_blk]
    outs = refs[n_blk : n_blk + n_sub]
    scratch = refs[n_blk + n_sub + (1 if extra else 0)]
    blk, sub = here[0], here[1]
    own = outs[0].shape[0]
    group = own // BS * n_sub
    scratch[...] = jnp.zeros_like(scratch)
    for d in range(n_blk):
        peer = blk ^ d
        for c in range(CAP):
            slot = peer * CAP + c
            alive = jnp.where(c < counts[peer], 1.0, 0.0).astype(F32)
            row = rows[slot] - blk * group
            scratch[rows_of(row)] += dot(
                tiles[slot] * alive, arrived[d][c * BS : (c + 1) * BS], ((1,), (0,))
            )
            ask = wanted[peer * CAP + c] - blk * group
            scratch[rows_of(ask)] += arrived[d][(CAP + c) * BS : (CAP + c + 1) * BS]
    for j in range(n_sub):
        outs[j][...] = scratch[rows_of(j ^ sub, own)]
    if extra:
        summed = refs[-1]
        for d in range(n_blk):
            summed[blk ^ d] = arrived[d][2 * CAP * BS :]
        total = summed[0]
        for d in range(1, n_blk):
            total = total + summed[d]
        refs[n_blk + n_sub][...] = total


def node_kernel(n_sub, scale, here, near, far, weight, bias, cotangent, *refs):
    activation, grad_spread = refs[0], refs[1]
    parts = refs[2 : 2 + n_sub]
    scratch = refs[-1]
    sub = here[1]
    spread = near[...] + far[...]
    pre = dot(spread, weight[...], ((1,), (0,))) + bias[...]
    sigma = jax.nn.sigmoid(pre)
    activation[...] = pre * sigma
    grad_pre = cotangent[...] * sigma * (1.0 + pre * (1.0 - sigma))
    grad_spread[...] = dot(grad_pre, weight[...], ((1,), (1,)))
    scratch[...] = dot(spread, grad_pre, ((0,), (0,))) * scale
    grad_bias = jnp.broadcast_to(jnp.sum(grad_pre, axis=0, keepdims=True) * scale, (PAD, BS))
    size = BS // n_sub
    for j in range(n_sub):
        parts[j][:size] = scratch[rows_of(j ^ sub, size)]
        parts[j][size:] = grad_bias


def end_kernel(n_sub, here, near, far, *refs):
    parts = refs[:n_sub]
    grad_features, grad_weight, grad_bias = refs[n_sub:]
    sub = here[1]
    size = BS // n_sub
    grad_features[...] = near[...] + far[...]
    for j in range(n_sub):
        grad_weight[rows_of(j ^ sub, size)] = parts[j][:size]
    grad_bias[...] = parts[0][size : size + 1]


def body(features, weight, bias, adj_tiles, tile_rows, tile_cols, tile_counts, cotangent):
    n_blk = lax.axis_size("blk")
    n_sub = lax.axis_size("sub")
    assert n_blk & (n_blk - 1) == 0 and n_sub & (n_sub - 1) == 0
    own, width = features.shape
    assert width == BS
    scale = 1.0 / math.sqrt(own * n_blk * n_sub)
    size = BS // n_sub + PAD
    here = jnp.stack([lax.axis_index("blk"), lax.axis_index("sub")]).astype(jnp.int32)
    wanted = lax.all_to_all(
        tile_cols.reshape(n_blk, CAP), "blk", split_axis=0, concat_axis=0, tiled=True
    ).reshape(-1)

    def shape(*dims):
        return jax.ShapeDtypeStruct(dims, F32)

    def call(kernel, scalars, arrays, outs, scratch):
        return pl.pallas_call(
            kernel,
            in_specs=[SMEM] * len(scalars) + [VMEM] * len(arrays),
            out_specs=[VMEM] * len(outs),
            out_shape=outs,
            scratch_shapes=[pltpu.VMEM(s, F32) for s in scratch],
            compiler_params=pltpu.CompilerParams(vmem_limit_bytes=56 << 20),
        )(*scalars, *arrays)

    def gather(value):
        held = {0: value}
        flip = n_sub // 2
        while flip:
            for j in list(held):
                held[j | flip] = swap(held[j], "sub", flip)
            flip //= 2
        return [held[j] for j in range(n_sub)]

    def aggregate(value, parts):
        extra = len(parts) > 0
        more = size if extra else 0
        scalars = (here, tile_rows, tile_counts, wanted)
        blocks = gather(value)
        if extra:
            parts = [parts[0]] + [swap(parts[j], "sub", j) for j in range(1, n_sub)]
        outgoing = call(
            functools.partial(send_kernel, n_blk, n_sub, extra),
            scalars,
            (adj_tiles, *blocks, *parts),
            [shape(2 * CAP * BS + more, width)] * n_blk,
            [(own * n_sub, width)] + ([(n_sub, size, width)] if extra else []),
        )
        arrived = [outgoing[0]] + [None] * (n_blk - 1)
        for d in range(n_blk - 1, 0, -1):
            arrived[d] = swap(outgoing[d], "blk", d)
        sums = call(
            functools.partial(sum_kernel, n_blk, n_sub, extra),
            scalars,
            (adj_tiles, *arrived),
            [shape(own, width)] * n_sub + ([shape(size, width)] if extra else []),
            [(own * n_sub, width)] + ([(n_blk, size, width)] if extra else []),
        )
        rest = sums[n_sub:]
        sums = list(sums[:n_sub])
        flip = 1
        pending = [None] * n_sub
        while flip < n_sub:
            for j in range(n_sub - 2 * flip, -1, -2 * flip):
                give = sums[j + flip]
                if pending[j + flip] is not None:
                    give = give + pending[j + flip]
                if pending[j] is not None:
                    sums[j] = sums[j] + pending[j]
                pending[j] = swap(give, "sub", flip)
            flip *= 2
        return sums[0], pending[0], rest

    near, far, _ = aggregate(features, ())
    activation, grad_spread, *parts = call(
        functools.partial(node_kernel, n_sub, scale),
        (here,),
        (near, far, weight, bias.reshape(1, width), cotangent),
        [shape(own, width)] * 2 + [shape(size, width)] * n_sub,
        [(BS, width)],
    )
    near, far, (total,) = aggregate(grad_spread, parts)
    quarters = [total] + [swap(total, "sub", j) for j in range(1, n_sub)]
    grad_features, grad_weight, grad_bias = call(
        functools.partial(end_kernel, n_sub),
        (here,),
        (near, far, *quarters),
        [shape(own, width), shape(BS, width), shape(1, width)],
        [],
    )
    return (activation, grad_features, grad_weight, grad_bias.reshape(width))


def solution(mesh):
    return jax.shard_map(
        body,
        mesh=mesh,
        in_specs=(
            P(("blk", "sub"), None),
            P(),
            P(),
            P(("blk", "sub"), None, None),
            P(("blk", "sub")),
            P(("blk", "sub")),
            P(("blk", "sub")),
            P(("blk", "sub"), None),
        ),
        out_specs=(P(("blk", "sub"), None), P(("blk", "sub"), None), P(), P()),
        check_vma=False,
    )
```

```python
import functools
import math

import jax
import jax.numpy as jnp
from jax import lax
from jax.experimental import pallas as pl
from jax.experimental.pallas import tpu as pltpu
from jax.sharding import PartitionSpec as P

BS = 128
CAP = 2
PAD = 8
HIGHEST = lax.Precision.HIGHEST
VMEM = pl.BlockSpec(memory_space=pltpu.VMEM)
SMEM = pl.BlockSpec(memory_space=pltpu.SMEM)
F32 = jnp.float32
BF16 = jnp.bfloat16


def dot(a, b, dims):
    return lax.dot_general(a, b, (dims, ((), ())), precision=HIGHEST, preferred_element_type=F32)


def halves(value):
    high = value.astype(BF16)
    low = (value - high.astype(F32)).astype(BF16)
    return jnp.concatenate([high, low], axis=0)


def tile_dot(tile, block):
    both = lax.dot_general(
        jnp.concatenate([tile, tile], axis=1),
        halves(block),
        (((1,), (0,)), ((), ())),
        preferred_element_type=F32,
    )
    return both[:BS] + both[BS:]


def swap(value, axis, flip):
    n = lax.axis_size(axis)
    return lax.ppermute(value, axis, [(i, i ^ flip) for i in range(n)])


def rows_of(index, size=BS):
    return pl.ds(pl.multiple_of(index * size, size), size)


def tile_kernel(counts, tiles, plain, flipped):
    @pl.loop(0, tiles.shape[0])
    def _(slot):
        alive = jnp.where(lax.rem(slot, CAP) < counts[lax.div(slot, CAP)], 1.0, 0.0).astype(F32)
        tile = tiles[slot] * alive
        plain[slot] = halves(tile)
        flipped[slot] = halves(tile.T)


def stage(here, blocks, group):
    for j, block in enumerate(blocks):
        own = block.shape[0]
        group[rows_of(j ^ here[1], own)] = block[...]


def product_kernel(n_sub, here, rows, flipped, *refs):
    blocks, outs, group = refs[:n_sub], refs[n_sub:-1], refs[-1]
    stage(here, blocks, group)
    base = here[0] * (group.shape[0] // BS)
    for d, out in enumerate(outs):
        peer = here[0] ^ d
        for c in range(CAP):
            row = rows[peer * CAP + c] - base
            out[c * BS : (c + 1) * BS] = tile_dot(flipped[peer * CAP + c], group[rows_of(row)])


def answer_kernel(n_sub, n_part, here, wanted, *refs):
    blocks, parts = refs[:n_sub], refs[n_sub : n_sub + n_part]
    scratch = 2 if n_part else 1
    outs, group = refs[n_sub + n_part : -scratch], refs[-scratch]
    stage(here, blocks, group)
    base = here[0] * (group.shape[0] // BS)
    if n_part:
        summed = refs[-1]
        for j, part in enumerate(parts):
            summed[j ^ here[1]] = part[...]
        total = summed[0]
        for j in range(1, n_part):
            total = total + summed[j]
    for d, out in enumerate(outs):
        peer = here[0] ^ d
        for c in range(CAP):
            out[c * BS : (c + 1) * BS] = group[rows_of(wanted[peer * CAP + c] - base)]
        if n_part:
            out[CAP * BS :] = total


def pull_kernel(n_blk, chained, extra, here, rows, plain, *refs):
    arrived, rest = refs[:n_blk], refs[n_blk:]
    acc = start_sums(chained, here, rest, 1 if extra else 0)
    base = here[0] * (acc.shape[0] // BS)
    for d in range(n_blk):
        peer = here[0] ^ d
        for c in range(CAP):
            row = rows[peer * CAP + c] - base
            acc[rows_of(row)] += tile_dot(
                plain[peer * CAP + c], arrived[d][c * BS : (c + 1) * BS]
            )
    if extra:
        summed, out = rest[-1], rest[-2]
        for d in range(n_blk):
            summed[here[0] ^ d] = arrived[d][CAP * BS :]
        total = summed[0]
        for d in range(1, n_blk):
            total = total + summed[d]
        out[...] = total
    if chained:
        finish_sums(here, acc, rest)


def push_kernel(n_blk, chained, here, wanted, *refs):
    arrived, rest = refs[:n_blk], refs[n_blk:]
    acc = start_sums(chained, here, rest, 0)
    base = here[0] * (acc.shape[0] // BS)
    for d in range(n_blk):
        peer = here[0] ^ d
        for c in range(CAP):
            ask = wanted[peer * CAP + c] - base
            acc[rows_of(ask)] += arrived[d][c * BS : (c + 1) * BS]
    if chained:
        finish_sums(here, acc, rest)


def start_sums(chained, here, rest, skip):
    if chained:
        acc = rest[-1]
        acc[...] = rest[0][...]
    else:
        acc = rest[0]
        acc[...] = jnp.zeros_like(acc)
    return acc


def finish_sums(here, acc, rest):
    for j, out in enumerate(rest[1:-1]):
        out[...] = acc[rows_of(j ^ here[1], out.shape[0])]


def node_kernel(n_sub, scale, here, near, far, weight, bias, cotangent, *refs):
    activation, grad_spread = refs[0], refs[1]
    parts = refs[2 : 2 + n_sub]
    scratch = refs[-1]
    spread = near[...] + far[...]
    pre = dot(spread, weight[...], ((1,), (0,))) + bias[...]
    sigma = jax.nn.sigmoid(pre)
    activation[...] = pre * sigma
    grad_pre = cotangent[...] * sigma * (1.0 + pre * (1.0 - sigma))
    grad_spread[...] = dot(grad_pre, weight[...], ((1,), (1,)))
    scratch[...] = dot(spread, grad_pre, ((0,), (0,))) * scale
    grad_bias = jnp.broadcast_to(jnp.sum(grad_pre, axis=0, keepdims=True) * scale, (PAD, BS))
    size = BS // n_sub
    for j in range(n_sub):
        parts[j][:size] = scratch[rows_of(j ^ here[1], size)]
        parts[j][size:] = grad_bias


def end_kernel(n_sub, here, near, far, *refs):
    parts = refs[:n_sub]
    grad_features, grad_weight, grad_bias = refs[n_sub:]
    size = BS // n_sub
    grad_features[...] = near[...] + far[...]
    for j in range(n_sub):
        grad_weight[rows_of(j ^ here[1], size)] = parts[j][:size]
    grad_bias[...] = parts[0][size : size + 1]


def body(features, weight, bias, adj_tiles, tile_rows, tile_cols, tile_counts, cotangent):
    n_blk = lax.axis_size("blk")
    n_sub = lax.axis_size("sub")
    assert n_blk & (n_blk - 1) == 0 and n_sub & (n_sub - 1) == 0
    own, width = features.shape
    slots = adj_tiles.shape[0]
    assert width == BS
    scale = 1.0 / math.sqrt(own * n_blk * n_sub)
    size = BS // n_sub + PAD
    here = jnp.stack([lax.axis_index("blk"), lax.axis_index("sub")]).astype(jnp.int32)

    def shape(*dims, kind=F32):
        return jax.ShapeDtypeStruct(dims, kind)

    def call(kernel, scalars, arrays, outs, scratch):
        held = sum(math.prod(a.shape) * a.dtype.itemsize for a in (*arrays, *outs))
        held += sum(math.prod(s) * 4 for s in scratch)
        return pl.pallas_call(
            kernel,
            in_specs=[SMEM] * len(scalars) + [VMEM] * len(arrays),
            out_specs=[VMEM] * len(outs),
            out_shape=outs,
            scratch_shapes=[pltpu.VMEM(s, F32) for s in scratch],
            compiler_params=pltpu.CompilerParams(vmem_limit_bytes=held + (2 << 20)),
        )(*scalars, *arrays)

    def gather(value):
        held = {0: value}
        flip = n_sub // 2
        while flip:
            for j in list(held):
                held[j | flip] = swap(held[j], "sub", flip)
            flip //= 2
        return [held[j] for j in range(n_sub)]

    def trade(outgoing):
        return [outgoing[0]] + [swap(outgoing[d], "blk", d) for d in range(1, n_blk)]

    group = (own * n_sub, width)
    sums_shape = [shape(own, width)] * n_sub

    def products(blocks):
        return call(
            functools.partial(product_kernel, n_sub),
            (here, tile_rows),
            (flipped, *blocks),
            [shape(CAP * BS, width)] * n_blk,
            [group],
        )

    def answers(blocks, parts):
        more = size if parts else 0
        return call(
            functools.partial(answer_kernel, n_sub, len(parts)),
            (here, wanted),
            (*blocks, *parts),
            [shape(CAP * BS + more, width)] * n_blk,
            [group] + ([(n_sub, size, width)] if parts else []),
        )

    def scatter(sums):
        sums = list(sums)
        flip = 1
        pending = [None] * n_sub
        while flip < n_sub:
            for j in range(n_sub - 2 * flip, -1, -2 * flip):
                give = sums[j + flip]
                if pending[j + flip] is not None:
                    give = give + pending[j + flip]
                if pending[j] is not None:
                    sums[j] = sums[j] + pending[j]
                pending[j] = swap(give, "sub", flip)
            flip *= 2
        return sums[0], pending[0]

    blocks = gather(features)
    wanted = lax.all_to_all(
        tile_cols.reshape(n_blk, CAP), "blk", split_axis=0, concat_axis=0, tiled=True
    ).reshape(-1)
    plain, flipped = call(
        tile_kernel,
        (tile_counts,),
        (adj_tiles,),
        [shape(slots, 2 * BS, BS, kind=BF16)] * 2,
        [],
    )
    out = products(blocks)
    pushed = trade(out)
    blocks, _ = lax.optimization_barrier((blocks, out[0]))
    pulled = trade(answers(blocks, []))
    acc = call(
        functools.partial(push_kernel, n_blk, False), (here, wanted), pushed, [shape(*group)], []
    )
    sums = call(
        functools.partial(pull_kernel, n_blk, True, False),
        (here, tile_rows),
        (plain, *pulled, *acc),
        sums_shape,
        [group],
    )
    near, far = scatter(sums)

    activation, grad_spread, *parts = call(
        functools.partial(node_kernel, n_sub, scale),
        (here,),
        (near, far, weight, bias.reshape(1, width), cotangent),
        [shape(own, width)] * 2 + [shape(size, width)] * n_sub,
        [(BS, width)],
    )

    blocks = gather(grad_spread)
    parts = parts[:1] + [swap(parts[j], "sub", j) for j in range(1, n_sub)]
    out = answers(blocks, parts)
    pulled = trade(out)
    blocks, _ = lax.optimization_barrier((blocks, out[0]))
    pushed = trade(products(blocks))
    *acc, total = call(
        functools.partial(pull_kernel, n_blk, False, True),
        (here, tile_rows),
        (plain, *pulled),
        [shape(*group), shape(size, width)],
        [(n_blk, size, width)],
    )
    quarters = [total] + [swap(total, "sub", j) for j in range(1, n_sub)]
    sums = call(
        functools.partial(push_kernel, n_blk, True),
        (here, wanted),
        (*pushed, *acc),
        sums_shape,
        [group],
    )
    near, far = scatter(sums)
    grad_features, grad_weight, grad_bias = call(
        functools.partial(end_kernel, n_sub),
        (here,),
        (near, far, *quarters),
        [shape(own, width), shape(BS, width), shape(1, width)],
        [],
    )
    return (activation, grad_features, grad_weight, grad_bias.reshape(width))


def solution(mesh):
    return jax.shard_map(
        body,
        mesh=mesh,
        in_specs=(
            P(("blk", "sub"), None),
            P(),
            P(),
            P(("blk", "sub"), None, None),
            P(("blk", "sub")),
            P(("blk", "sub")),
            P(("blk", "sub")),
            P(("blk", "sub"), None),
        ),
        out_specs=(P(("blk", "sub"), None), P(("blk", "sub"), None), P(), P()),
        check_vma=False,
    )
```

```python
import functools
import math

import jax
import jax.numpy as jnp
from jax import lax
from jax.experimental import pallas as pl
from jax.experimental.pallas import tpu as pltpu
from jax.sharding import PartitionSpec as P


BS = 128
CAP = 2
PAD = 8
HIGHEST = lax.Precision.HIGHEST
VMEM = pl.BlockSpec(memory_space=pltpu.VMEM)
SMEM = pl.BlockSpec(memory_space=pltpu.SMEM)
F32 = jnp.float32
BF16 = jnp.bfloat16


def dot(a, b, dims):
    return lax.dot_general(a, b, (dims, ((), ())), precision=HIGHEST, preferred_element_type=F32)


def halves(value):
    high = value.astype(BF16)
    low = (value - high.astype(F32)).astype(BF16)
    return jnp.concatenate([high, low], axis=0)


def tile_dot(tile, block):
    both = lax.dot_general(
        jnp.concatenate([tile, tile], axis=1),
        halves(block),
        (((1,), (0,)), ((), ())),
        preferred_element_type=F32,
    )
    return both[:BS] + both[BS:]


def swap(value, axis, flip):
    n = lax.axis_size(axis)
    return lax.ppermute(value, axis, [(i, i ^ flip) for i in range(n)])


def rows_of(index, size=BS):
    return pl.ds(pl.multiple_of(index * size, size), size)


def tile_kernel(counts, tiles, plain, flipped):
    for i in range(tiles.shape[0]):
        slot = pl.program_id(0) * tiles.shape[0] + i
        alive = jnp.where(lax.rem(slot, CAP) < counts[lax.div(slot, CAP)], 1.0, 0.0).astype(F32)
        tile = tiles[i] * alive
        plain[i] = halves(tile)
        flipped[i] = halves(tile.T)


def stage(here, blocks, group):
    for j, block in enumerate(blocks):
        own = block.shape[0]
        group[rows_of(j ^ here[1], own)] = block[...]


def product_kernel(n_sub, here, rows, flipped, *refs):
    blocks, outs, group = refs[:n_sub], refs[n_sub:-1], refs[-1]
    stage(here, blocks, group)
    base = here[0] * (group.shape[0] // BS)
    for d, out in enumerate(outs):
        peer = here[0] ^ d
        for c in range(CAP):
            row = rows[peer * CAP + c] - base
            out[c * BS : (c + 1) * BS] = tile_dot(flipped[peer * CAP + c], group[rows_of(row)])


def answer_kernel(n_sub, n_part, here, wanted, *refs):
    blocks, parts = refs[:n_sub], refs[n_sub : n_sub + n_part]
    scratch = 2 if n_part else 1
    outs, group = refs[n_sub + n_part : -scratch], refs[-scratch]
    stage(here, blocks, group)
    base = here[0] * (group.shape[0] // BS)
    if n_part:
        summed = refs[-1]
        for j, part in enumerate(parts):
            summed[j ^ here[1]] = part[...]
        total = summed[0]
        for j in range(1, n_part):
            total = total + summed[j]
    for d, out in enumerate(outs):
        peer = here[0] ^ d
        for c in range(CAP):
            out[c * BS : (c + 1) * BS] = group[rows_of(wanted[peer * CAP + c] - base)]
        if n_part:
            out[CAP * BS :] = total


def pull_kernel(n_blk, chained, extra, here, rows, plain, *refs):
    arrived, rest = refs[:n_blk], refs[n_blk:]
    acc = start_sums(chained, rest)
    base = here[0] * (acc.shape[0] // BS)
    for d in range(n_blk):
        peer = here[0] ^ d
        for c in range(CAP):
            row = rows[peer * CAP + c] - base
            acc[rows_of(row)] += tile_dot(
                plain[peer * CAP + c], arrived[d][c * BS : (c + 1) * BS]
            )
    if extra:
        summed, out = rest[-1], rest[-2]
        for d in range(n_blk):
            summed[here[0] ^ d] = arrived[d][CAP * BS :]
        total = summed[0]
        for d in range(1, n_blk):
            total = total + summed[d]
        out[...] = total
    if chained:
        finish_sums(here, acc, rest)


def push_kernel(n_blk, chained, here, wanted, *refs):
    arrived, rest = refs[:n_blk], refs[n_blk:]
    acc = start_sums(chained, rest)
    base = here[0] * (acc.shape[0] // BS)
    for d in range(n_blk):
        peer = here[0] ^ d
        for c in range(CAP):
            ask = wanted[peer * CAP + c] - base
            acc[rows_of(ask)] += arrived[d][c * BS : (c + 1) * BS]
    if chained:
        finish_sums(here, acc, rest)


def start_sums(chained, rest):
    if chained:
        acc = rest[-1]
        acc[...] = rest[0][...]
    else:
        acc = rest[0]
        acc[...] = jnp.zeros_like(acc)
    return acc


def finish_sums(here, acc, rest):
    for j, out in enumerate(rest[1:-1]):
        out[...] = acc[rows_of(j ^ here[1], out.shape[0])]


def node_kernel(n_sub, scale, here, near, far, weight, bias, cotangent, *refs):
    activation, grad_spread = refs[0], refs[1]
    parts = refs[2 : 2 + n_sub]
    scratch = refs[-1]
    spread = near[...] + far[...]
    pre = dot(spread, weight[...], ((1,), (0,))) + bias[...]
    sigma = jax.nn.sigmoid(pre)
    activation[...] = pre * sigma
    grad_pre = cotangent[...] * sigma * (1.0 + pre * (1.0 - sigma))
    grad_spread[...] = dot(grad_pre, weight[...], ((1,), (1,)))
    scratch[...] = dot(spread, grad_pre, ((0,), (0,))) * scale
    grad_bias = jnp.broadcast_to(jnp.sum(grad_pre, axis=0, keepdims=True) * scale, (PAD, BS))
    size = BS // n_sub
    for j in range(n_sub):
        parts[j][:size] = scratch[rows_of(j ^ here[1], size)]
        parts[j][size:] = grad_bias


def end_kernel(n_sub, here, near, far, *refs):
    parts = refs[:n_sub]
    grad_features, grad_weight, grad_bias = refs[n_sub:]
    size = BS // n_sub
    grad_features[...] = near[...] + far[...]
    for j in range(n_sub):
        grad_weight[rows_of(j ^ here[1], size)] = parts[j][:size]
    grad_bias[...] = parts[0][size : size + 1]


def body(features, weight, bias, adj_tiles, tile_rows, tile_cols, tile_counts, cotangent):
    n_blk = lax.axis_size("blk")
    n_sub = lax.axis_size("sub")
    assert n_blk & (n_blk - 1) == 0 and n_sub & (n_sub - 1) == 0
    own, width = features.shape
    slots = adj_tiles.shape[0]
    assert width == BS
    scale = 1.0 / math.sqrt(own * n_blk * n_sub)
    size = BS // n_sub + PAD
    here = jnp.stack([lax.axis_index("blk"), lax.axis_index("sub")]).astype(jnp.int32)

    def shape(*dims, kind=F32):
        return jax.ShapeDtypeStruct(dims, kind)

    def call(kernel, scalars, arrays, outs, scratch):
        held = sum(math.prod(a.shape) * a.dtype.itemsize for a in (*arrays, *outs))
        held += sum(math.prod(s) * 4 for s in scratch)
        return pl.pallas_call(
            kernel,
            in_specs=[SMEM] * len(scalars) + [VMEM] * len(arrays),
            out_specs=[VMEM] * len(outs),
            out_shape=outs,
            scratch_shapes=[pltpu.VMEM(s, F32) for s in scratch],
            compiler_params=pltpu.CompilerParams(vmem_limit_bytes=held + (2 << 20)),
        )(*scalars, *arrays)

    def gather(value):
        held = {0: value}
        flip = n_sub // 2
        while flip:
            for j in list(held):
                held[j | flip] = swap(held[j], "sub", flip)
            flip //= 2
        return [held[j] for j in range(n_sub)]

    def trade(outgoing):
        return [outgoing[0]] + [swap(outgoing[d], "blk", d) for d in range(1, n_blk)]

    group = (own * n_sub, width)
    sums_shape = [shape(own, width)] * n_sub

    def products(blocks):
        return call(
            functools.partial(product_kernel, n_sub),
            (here, tile_rows),
            (flipped, *blocks),
            [shape(CAP * BS, width)] * n_blk,
            [group],
        )

    def answers(blocks, parts):
        more = size if parts else 0
        return call(
            functools.partial(answer_kernel, n_sub, len(parts)),
            (here, wanted),
            (*blocks, *parts),
            [shape(CAP * BS + more, width)] * n_blk,
            [group] + ([(n_sub, size, width)] if parts else []),
        )

    def scatter(sums):
        sums = list(sums)
        flip = 1
        pending = [None] * n_sub
        while flip < n_sub:
            for j in range(n_sub - 2 * flip, -1, -2 * flip):
                give = sums[j + flip]
                if pending[j + flip] is not None:
                    give = give + pending[j + flip]
                if pending[j] is not None:
                    sums[j] = sums[j] + pending[j]
                pending[j] = swap(give, "sub", flip)
            flip *= 2
        return sums[0], pending[0]

    blocks = gather(features)
    wanted = lax.all_to_all(
        tile_cols.reshape(n_blk, CAP), "blk", split_axis=0, concat_axis=0, tiled=True
    )
    step = 4 if slots % 4 == 0 else 1
    whole = pl.BlockSpec((step, 2 * BS, BS), lambda i: (i, 0, 0))
    plain, flipped = pl.pallas_call(
        tile_kernel,
        grid=(slots // step,),
        in_specs=[SMEM, pl.BlockSpec((step, BS, BS), lambda i: (i, 0, 0))],
        out_specs=[whole, whole],
        out_shape=[shape(slots, 2 * BS, BS, kind=BF16)] * 2,
        compiler_params=pltpu.CompilerParams(vmem_limit_bytes=8 << 20),
    )(tile_counts, adj_tiles)
    out = products(blocks)
    pushed = trade(out)
    wanted = wanted.reshape(-1)
    pulled = trade(answers(blocks, []))
    acc = call(
        functools.partial(push_kernel, n_blk, False), (here, wanted), pushed, [shape(*group)], []
    )
    sums = call(
        functools.partial(pull_kernel, n_blk, True, False),
        (here, tile_rows),
        (plain, *pulled, *acc),
        sums_shape,
        [group],
    )
    near, far = scatter(sums)

    activation, grad_spread, *parts = call(
        functools.partial(node_kernel, n_sub, scale),
        (here,),
        (near, far, weight, bias.reshape(1, width), cotangent),
        [shape(own, width)] * 2 + [shape(size, width)] * n_sub,
        [(BS, width)],
    )

    blocks = gather(grad_spread)
    parts = parts[:1] + [swap(parts[j], "sub", j) for j in range(1, n_sub)]
    out = answers(blocks, parts)
    pulled = trade(out)
    pushed = trade(products(blocks))
    *acc, total = call(
        functools.partial(pull_kernel, n_blk, False, True),
        (here, tile_rows),
        (plain, *pulled),
        [shape(*group), shape(size, width)],
        [(n_blk, size, width)],
    )
    quarters = [total] + [swap(total, "sub", j) for j in range(1, n_sub)]
    sums = call(
        functools.partial(push_kernel, n_blk, True),
        (here, wanted),
        (*pushed, *acc),
        sums_shape,
        [group],
    )
    near, far = scatter(sums)
    grad_features, grad_weight, grad_bias = call(
        functools.partial(end_kernel, n_sub),
        (here,),
        (near, far, *quarters),
        [shape(own, width), shape(BS, width), shape(1, width)],
        [],
    )
    return (activation, grad_features, grad_weight, grad_bias.reshape(width))


def solution(mesh):
    return jax.shard_map(
        body,
        mesh=mesh,
        in_specs=(
            P(("blk", "sub"), None),
            P(),
            P(),
            P(("blk", "sub"), None, None),
            P(("blk", "sub")),
            P(("blk", "sub")),
            P(("blk", "sub")),
            P(("blk", "sub"), None),
        ),
        out_specs=(P(("blk", "sub"), None), P(("blk", "sub"), None), P(), P()),
        check_vma=False,
    )
```
